256 devices in a mesh: seq: 32 (over x, y, core), head: 8 (over z).
Axes of the slice: x: 4, y: 4, z: 8, core: 2. Of those that a mesh axis runs over, the one named last changes fastest.
Arguments:
- queries: bfloat16 [32768, 1024], P('seq', 'head'), may hold values from -6 to 6
- values: bfloat16 [32768, 1024], P('seq', 'head'), may hold values from -6 to 6
- w_out: bfloat16 [1024, 1024], P('head'), may hold values from -0.1875 to 0.1875
- out_grad: bfloat16 [32768, 1024], P('seq', 'head'), may hold values from -6 to 6
- slots: int32 [2, 16, 32768], P(None, 'head', 'seq'), may hold values from 0 to 32767, as said below
Outputs:
- output: bfloat16 [32768, 1024], P('seq', 'head')
- query_grad: bfloat16 [32768, 1024], P('seq', 'head')
- value_grad: bfloat16 [32768, 1024], P('seq', 'head')
- w_out_grad: float32 [1024, 1024], P('head')
The draws below stay inside these ranges and needn't reach their ends.
Inputs may be any that keep to these rules, and one draw needn't show every extreme that they name: slots[r, h] is a permutation of the token positions: each token's place in round r's stable sort of head h's bucket ids. Of the 1024 tokens of one device of seq, exactly 48 have places among the 1024 places of one device of seq (possibly itself), 16 among those of the next device cyclically, and 32 among those of each other device.
All inputs are finite; a program needn't handle non-finite values.
Results may differ from the reference program's by a relative error of at most 0.024.
Values may be sent and summed in bfloat16 or wider, within the bound.
A program may use at most 64 MiB of HBM per device.

```python
import jax
import jax.numpy as jnp
from jax import lax

D = 1024
HEADS = 16
DH = 64
ROUNDS = 2
SPAN = 128
TOK_DEV = 1024
TOKENS = 32768
N_HEAD = 8


def draw_slots(key, part):
    shard_count = TOKENS // TOK_DEV
    even_share = TOK_DEV // shard_count
    token_index = jnp.arange(TOK_DEV, dtype=jnp.int32)
    labels = token_index // even_share
    global_index = jnp.arange(TOKENS, dtype=jnp.int32)

    def draw_single(seed_key):
        first_key, second_key, third_key = jax.random.split(seed_key, 3)
        heavy_target = jax.random.permutation(first_key, shard_count).astype(jnp.int32)
        light_target = (heavy_target + 1) % shard_count
        base_labels = jnp.broadcast_to(labels[None, :], (shard_count, TOK_DEV))
        moved_mask = (base_labels == light_target[:, None]) & ((token_index % even_share)[None, :] < even_share // 2)
        shaped_labels = jnp.where(moved_mask, heavy_target[:, None], base_labels)
        row_keys = jax.random.split(second_key, shard_count)
        shuffled = jax.vmap(jax.random.permutation)(row_keys, shaped_labels)
        destination = shuffled.reshape(TOKENS).astype(jnp.int32)
        bucket = jax.random.randint(third_key, (TOKENS,), 0, 64, dtype=jnp.int32)
        sort_key = (destination * 64 + bucket) * TOKENS + global_index
        sort_order = jnp.argsort(sort_key)
        return jnp.zeros((TOKENS,), jnp.int32).at[sort_order].set(global_index)
    seed_keys = jax.random.split(key, ROUNDS * HEADS)
    return jax.vmap(draw_single)(seed_keys).reshape(ROUNDS, HEADS, TOKENS)


def block_levels(own_key, extent, pieces, least, largest):
    def one(axis_at, parts):
        steps = jax.random.uniform(jax.random.fold_in(jax.random.fold_in(own_key, 6), axis_at), (parts,), jnp.float32, least / len(pieces), largest / len(pieces))
        return jnp.repeat(jnp.exp(steps), extent[axis_at] // parts).reshape((-1,) + (1,) * (len(extent) - axis_at - 1))

    level = one(*pieces[0])
    for cut in pieces[1:]:
        level = level * one(*cut)
    return level


def normal_values(key, extent, deviation, bound, cuts=(), kind=jnp.bfloat16):
    level = block_levels(key, extent, cuts, -0.22, 0.18) if cuts else 1.0
    values = jax.random.normal(key, extent, jnp.float32) * deviation * level
    return jnp.minimum(jnp.maximum(values, -bound), bound).astype(kind)


def setup_inputs(seed: int = 0) -> dict:
    key_of = jax.random.split(jax.random.key(seed), 6)
    return {
        "queries": normal_values(key_of[0], (TOKENS, HEADS * DH), 1.0, 6.0, ((0, 32), (1, 8))),
        "values": normal_values(key_of[1], (TOKENS, HEADS * DH), 1.0, 6.0, ((0, 32), (1, 8))),
        "w_out": normal_values(key_of[2], (HEADS * DH, D), (HEADS * DH) ** -0.5, 0.1875, ((0, 8),)),
        "out_grad": normal_values(key_of[3], (TOKENS, D), 1.0, 6.0, ((0, 32), (1, 8))),
        "slots": draw_slots(jax.random.fold_in(key_of[5], 71), 0),
    }


def window_of(blocks):
    return jnp.concatenate([blocks, jnp.roll(blocks, 1, axis=0)], axis=1)

def round_forward(query_rows, value_rows, slot_row):
    token_count = query_rows.shape[0]
    head_width = query_rows.shape[1]
    score_scale = head_width ** (-0.5)
    positions = jnp.arange(token_count, dtype=jnp.int32)
    sorted_query = jnp.zeros_like(query_rows).at[slot_row].set(query_rows)
    sorted_value = jnp.zeros_like(value_rows).at[slot_row].set(value_rows)
    sorted_place = jnp.zeros((token_count,), jnp.int32).at[slot_row].set(positions)
    block_count = token_count // SPAN
    query_float = sorted_query.astype(jnp.float32)
    inverse = lax.rsqrt(lax.optimization_barrier(jnp.mean(query_float * query_float, axis=-1, keepdims=True)) + 1e-06)
    sorted_key = (query_float * inverse).astype(jnp.bfloat16)
    query_blocks = sorted_query.reshape(block_count, SPAN, head_width)
    key_window = window_of(sorted_key.reshape(block_count, SPAN, head_width))
    value_window = window_of(sorted_value.reshape(block_count, SPAN, head_width))
    place_blocks = sorted_place.reshape(block_count, SPAN)
    place_window = window_of(place_blocks)
    raw_scores = jnp.einsum('cqd,ckd->cqk', query_blocks.astype(jnp.float32), key_window.astype(jnp.float32)) * score_scale
    own_token = (jnp.arange(SPAN)[:, None] == jnp.arange(2 * SPAN)[None, :]).astype(jnp.float32)
    future = (place_window[:, None, :] > place_blocks[:, :, None]).astype(jnp.float32)
    scores = raw_scores - 100000.0 * own_token - 1000000000.0 * future
    row_top = lax.optimization_barrier(jnp.max(scores, axis=-1))
    log_total = row_top + jnp.log(lax.optimization_barrier(jnp.sum(jnp.exp(scores - row_top[..., None]), axis=-1)))
    weights = jnp.exp(scores - log_total[..., None])
    rounded_probs = weights.astype(jnp.bfloat16)
    block_out = jnp.einsum('cqk,ckd->cqd', rounded_probs.astype(jnp.float32), value_window.astype(jnp.float32)).astype(jnp.bfloat16)
    token_out = block_out.reshape(token_count, head_width)[slot_row]
    token_log = log_total.reshape(token_count)[slot_row]
    saved = (query_blocks, key_window, value_window, weights, rounded_probs, query_float, inverse)
    return (saved, token_out, token_log)

def round_backward(saved, grad_rows, delta_rows, slot_row):
    query_blocks, key_window, value_window, weights, rounded_probs, query_float, inverse = saved
    token_count = grad_rows.shape[0]
    head_width = grad_rows.shape[1]
    score_scale = head_width ** (-0.5)
    block_count = token_count // SPAN
    sorted_grad = jnp.zeros_like(grad_rows).at[slot_row].set(grad_rows)
    sorted_delta = jnp.zeros((token_count,), jnp.float32).at[slot_row].set(delta_rows)
    grad_blocks = sorted_grad.reshape(block_count, SPAN, head_width)
    delta_blocks = sorted_delta.reshape(block_count, SPAN)
    dot_grad = jnp.einsum('cqd,ckd->cqk', grad_blocks.astype(jnp.float32), value_window.astype(jnp.float32))
    score_grad = (weights * (dot_grad - delta_blocks[..., None])).astype(jnp.bfloat16)
    query_part = jnp.einsum('cqk,ckd->cqd', score_grad.astype(jnp.float32), key_window.astype(jnp.float32)) * score_scale
    key_part = jnp.einsum('cqk,cqd->ckd', score_grad.astype(jnp.float32), query_blocks.astype(jnp.float32)) * score_scale
    value_part = jnp.einsum('cqk,cqd->ckd', rounded_probs.astype(jnp.float32), grad_blocks.astype(jnp.float32))
    key_grad = key_part[:, :SPAN] + jnp.roll(key_part[:, SPAN:], -1, axis=0)
    value_sum = value_part[:, :SPAN] + jnp.roll(value_part[:, SPAN:], -1, axis=0)
    key_grad = key_grad.reshape(token_count, head_width)
    value_sum = value_sum.reshape(token_count, head_width)
    query_total = query_part.reshape(token_count, head_width) + inverse * key_grad - query_float * (inverse * inverse * inverse) * lax.optimization_barrier(jnp.mean(query_float * key_grad, axis=-1, keepdims=True))
    return (query_total.astype(jnp.bfloat16)[slot_row], value_sum.astype(jnp.bfloat16)[slot_row])

def reference(queries, values, w_out, out_grad, slots):
    token_count = queries.shape[0]
    head_width = DH
    back_full = jnp.dot(out_grad, w_out.T, preferred_element_type=jnp.float32).astype(jnp.bfloat16)
    attention_columns = []
    query_columns = []
    value_columns = []
    for head_index in range(HEADS):
        first_column = head_index * head_width
        query_rows = queries[:, first_column:first_column + head_width]
        value_rows = values[:, first_column:first_column + head_width]
        results = [round_forward(query_rows, value_rows, slots[turn_index, head_index]) for turn_index in range(ROUNDS)]
        log_stack = jnp.stack([result_entry[2] for result_entry in results])
        mixing = jax.nn.softmax(log_stack, axis=0)
        combined = jnp.zeros((token_count, head_width), jnp.float32)
        for turn_index in range(ROUNDS):
            combined = combined + mixing[turn_index][:, None] * results[turn_index][1].astype(jnp.float32)
        attention_columns.append(combined.astype(jnp.bfloat16))
        back_head = back_full[:, first_column:first_column + head_width].astype(jnp.float32)
        inner_rows = lax.optimization_barrier(jnp.sum(back_head * combined, axis=-1))
        query_sum = jnp.zeros((token_count, head_width), jnp.float32)
        value_sum = jnp.zeros((token_count, head_width), jnp.float32)
        for turn_index in range(ROUNDS):
            grad_rows = (mixing[turn_index][:, None] * back_head).astype(jnp.bfloat16)
            delta_rows = mixing[turn_index] * inner_rows
            query_part, value_part = round_backward(results[turn_index][0], grad_rows, delta_rows, slots[turn_index, head_index])
            query_sum = query_sum + query_part.astype(jnp.float32)
            value_sum = value_sum + value_part.astype(jnp.float32)
        query_columns.append(query_sum.astype(jnp.bfloat16))
        value_columns.append(value_sum.astype(jnp.bfloat16))
    attention = jnp.concatenate(attention_columns, axis=1)
    group_width = HEADS * DH // N_HEAD
    mixed = jnp.zeros((token_count, D), jnp.float32)
    for member in range(N_HEAD):
        partial_value = jnp.dot(attention[:, member * group_width:(member + 1) * group_width], w_out[member * group_width:(member + 1) * group_width], preferred_element_type=jnp.float32).astype(jnp.bfloat16)
        partial_value = lax.optimization_barrier(partial_value)
        mixed = mixed + partial_value.astype(jnp.float32)
    output = mixed.astype(jnp.bfloat16)
    w_out_grad = jnp.dot(attention.T, out_grad, preferred_element_type=jnp.float32) * token_count ** (-0.5)
    query_grad = jnp.concatenate(query_columns, axis=1)
    value_grad = jnp.concatenate(value_columns, axis=1)
    return (output, query_grad, value_grad, w_out_grad)
```

```python
import functools

import jax
import jax.numpy as jnp
from jax import lax
from jax.experimental import pallas as pl
from jax.experimental.pallas import tpu as pltpu
from jax.sharding import PartitionSpec as P

DH = 64
SPAN = 128
WIDE = 2 * DH
ROUNDS = 2
PAIR = 2
EXTRA = 16
PEERS = 4
MESH = pl.DeviceIdType.MESH
F32 = jnp.float32
BF16 = jnp.bfloat16
I32 = jnp.int32


def iota(shape, dim):
    return lax.broadcasted_iota(I32, shape, dim)


def one_hot(mask):
    return jnp.where(mask, 1.0, 0.0).astype(BF16)


def dot(a, b):
    return jnp.dot(a, b, preferred_element_type=F32)


def dot_nt(a, b):
    return lax.dot_general(a, b, (((1,), (1,)), ((), ())), preferred_element_type=F32)


def dot_tn(a, b):
    return lax.dot_general(a, b, (((0,), (0,)), ((), ())), preferred_element_type=F32)


def to_row(col):
    eye = iota((SPAN, SPAN), 0) == iota((SPAN, SPAN), 1)
    return jnp.sum(jnp.where(eye, col, 0.0), axis=0, keepdims=True)


def swap_halves(x):
    return pltpu.roll(x, DH, 1)


def split3(x):
    top = x.astype(BF16).astype(F32)
    rest = x - top
    middle = rest.astype(BF16).astype(F32)
    return [top, middle, rest - middle]


def kernel(
    n, z,
    q_ref, v_ref, w_ref, g_ref, slots_ref,
    out_ref, dq_ref, dv_ref, dw_ref,
    send1, recv1, send2, recv2, send3, recv3, send4, recv4,
    xqv, comb_row, comb_col, slot_row, slot_col, place_col, dest_row, place_row,
    ext, keys, inv_col, probs, log_row, outs, back, attn, attn_t, grads, delta_row,
    sorted_grad, delta_col, query_part, key_value, final, spill_out, spill_in, own_grads,
    full_grad, terms, up_in, down_in, wsend, wrecv, wsum, wall,
    ssem, rsem, bsend, brecv, psend, precv, gus, gur, gds, gdr, rus, rur, rds, rdr, wss, wrs,
):
    rows = q_ref.shape[0]
    share = rows // n
    cap = share * 3 // 2
    total = n * cap
    log_rows = rows.bit_length() - 1
    nb = rows // SPAN
    up_steps = z // 2
    down_steps = z - 1 - up_steps
    tiles = n // PEERS
    tile = PEERS * cap
    me = lax.axis_index("seq")
    me_h = lax.axis_index("head")
    up, down = lax.rem(me_h + 1, z), lax.rem(me_h + z - 1, z)
    after, before = lax.rem(me + 1, n), lax.rem(me + n - 1, n)

    barrier = pltpu.get_barrier_semaphore()

    def greet(off, carry):
        pl.semaphore_signal(barrier, inc=1, device_id={"seq": lax.rem(me + off, n)}, device_id_type=MESH)
        return carry

    lax.fori_loop(1, n, greet, 0)
    pl.semaphore_signal(barrier, inc=1, device_id={"head": up}, device_id_type=MESH)
    pl.semaphore_signal(barrier, inc=1, device_id={"head": down}, device_id_type=MESH)

    def exchange_start(send, recv, send_sem, recv_sem):
        def one(off, carry):
            peer = lax.rem(me + off, n)
            pltpu.make_async_remote_copy(
                send.at[peer], recv.at[me], send_sem, recv_sem, device_id={"seq": peer}, device_id_type=MESH
            ).start()
            return carry

        pltpu.make_async_copy(send.at[me], recv.at[me], recv_sem).start()
        lax.fori_loop(1, n, one, 0)

    def exchange_wait(recv, recv_sem):
        pltpu.make_async_copy(recv, recv, recv_sem).wait()

    def exchange_drain(send, send_sem):
        part = send.at[pl.ds(0, n - 1)]
        pltpu.make_async_copy(part, part, send_sem).wait()

    def gather_copy(going_up, step):
        if going_up:
            slot, sems, peer = lax.rem(me_h - (step - 1) + z, z), (gus, gur), up
        else:
            slot, sems, peer = lax.rem(me_h + (step - 1), z), (gds, gdr), down
        return pltpu.make_async_remote_copy(
            full_grad.at[slot], full_grad.at[slot], sems[0].at[step - 1], sems[1].at[step - 1],
            device_id={"head": peer}, device_id_type=MESH,
        )

    def gather_wait(going_up, step):
        slot = lax.rem(me_h - step + z, z) if going_up else lax.rem(me_h + step, z)
        sem = (gur if going_up else gdr).at[step - 1]
        pltpu.make_async_copy(full_grad.at[slot], full_grad.at[slot], sem).wait()

    def gather_step(step):
        for going_up, steps in ((True, up_steps), (False, down_steps)):
            if 1 < step <= steps + 1:
                gather_wait(going_up, step - 1)
            if step <= steps:
                gather_copy(going_up, step).start()

    def messages(comps, base):
        sub = iota((n, EXTRA, WIDE), 1)
        value = jnp.zeros((n, EXTRA, WIDE), F32)
        for at in range(comps):
            value = jnp.where(sub == at, base[at * n : (at + 1) * n][:, None, :], value)
        return value.astype(BF16)

    def message_parts(ref_value, comps):
        sub = iota((n, EXTRA, WIDE), 1)
        value = ref_value.astype(F32)
        return [jnp.sum(jnp.where(sub == at, value, 0.0), axis=1) for at in range(comps)]

    def scatter_small(parts, turn, target, spot):
        hot = jnp.where(iota((n, rows), 0) == target, 1.0, 0.0)
        left = jnp.concatenate([hot * part for part in parts], axis=0).astype(BF16)
        right = one_hot(iota((WIDE, rows), 0) == spot + DH * turn)
        return dot_nt(left, right)

    def gather_small(parts, turn, target, spot):
        hot = one_hot(iota((SPAN, n), 1) == target)
        wide = dot(hot, parts)
        value = wide[:, :WIDE] + wide[:, WIDE : 2 * WIDE] + wide[:, 2 * WIDE :]
        chosen = iota((SPAN, WIDE), 1) == spot + DH * turn
        return jnp.sum(jnp.where(chosen, value, 0.0), axis=1, keepdims=True)

    low_half = iota((SPAN, WIDE), 1) < DH

    for head in range(PAIR):
        for at in range(nb):
            sl = pl.ds(at * SPAN, SPAN)
            query = q_ref[sl, :].astype(F32)
            value = v_ref[sl, :].astype(F32)
            if head == 0:
                xqv[head, sl, :] = jnp.where(low_half, query, swap_halves(value)).astype(BF16)
            else:
                xqv[head, sl, :] = jnp.where(low_half, swap_halves(query), value).astype(BF16)
    full_grad[me_h] = g_ref[...]

    hots = []
    for head in range(PAIR):
        for turn in range(ROUNDS):
            slot = slots_ref[turn * PAIR + head : turn * PAIR + head + 1, :]
            hots.append(jnp.where(iota((n, rows), 0) == (slot >> log_rows), 1.0, 0.0))
    hot = jnp.concatenate(hots, axis=0)
    ahead = one_hot(iota((SPAN, SPAN), 0) < iota((SPAN, SPAN), 1))
    carry = jnp.zeros((4 * n, 1), F32)
    ranks = [[] for _ in range(4)]
    for at in range(nb):
        part = hot[:, at * SPAN : (at + 1) * SPAN]
        count = (dot(part.astype(BF16), ahead) + carry) * part
        carry = carry + jnp.sum(part, axis=1, keepdims=True)
        for b in range(4):
            ranks[b].append(jnp.sum(count[b * n : (b + 1) * n], axis=0, keepdims=True))
    position = iota((1, rows), 1)
    for head in range(PAIR):
        base = jnp.zeros((4 * n, WIDE), F32)
        for turn in range(ROUNDS):
            b = 2 * head + turn
            slot = slots_ref[turn * PAIR + head : turn * PAIR + head + 1, :]
            target = slot >> log_rows
            rank = jnp.concatenate(ranks[b], axis=1)
            rank_int = rank.astype(I32)
            comb = target * DH + rank_int
            comb_row[b] = comb
            comb_col[b] = jnp.transpose(jnp.broadcast_to(comb.astype(F32), (8, rows)))[:, :1].astype(I32)
            place = (slot & (rows - 1)) + 1
            parts = [place >> 5, place & 31, position >> 5, position & 31]
            base = base + scatter_small([p.astype(F32) for p in parts], turn, target, rank_int)
        send1[head, :, 2 * cap : 2 * cap + EXTRA, :] = messages(4, base)

    pl.semaphore_wait(barrier, n + 1)
    gather_step(1)

    def spot_rows(b):
        comb = comb_row[b]
        return (comb >> 6) * cap + (comb & (DH - 1))

    def pack_head(head, carry):
        def pack_tile(at, inner):
            line = iota((tile, rows), 0) + at * tile
            for turn in range(ROUNDS):
                hot = one_hot(line == spot_rows(2 * head + turn))
                moved = dot(hot, xqv[head]).astype(BF16).reshape(PEERS, cap, WIDE)
                send1[head, pl.ds(at * PEERS, PEERS), turn * cap : (turn + 1) * cap, :] = moved
            return inner

        lax.fori_loop(0, tiles, pack_tile, 0)
        exchange_start(send1.at[head], recv1.at[head], ssem.at[0, head], rsem.at[0, head])
        return carry

    lax.fori_loop(0, PAIR, pack_head, 0)
    gather_step(2)

    lanes = iota((1, total), 1)
    source = jnp.floor((lanes.astype(F32) + 0.5) * (1.0 / cap)).astype(I32)
    within = lanes - source * cap

    def boundary_copies(head):
        copies = []
        for turn in range(ROUNDS):
            b = 2 * head + turn
            copies.append((ext.at[b, pl.ds(rows, SPAN)], ext.at[b, pl.ds(0, SPAN)]))
        copies.append((place_row.at[head, nb], place_row.at[head, 0]))
        return [
            pltpu.make_async_remote_copy(
                src, dst, bsend.at[head, at], brecv.at[head, at], device_id={"seq": after}, device_id_type=MESH
            )
            for at, (src, dst) in enumerate(copies)
        ]

    def sort_head(head, carry):
        exchange_wait(recv1.at[head], rsem.at[0, head])
        info = message_parts(recv1[head, :, 2 * cap : 2 * cap + EXTRA, :], 4)
        info = jnp.concatenate(info, axis=0).astype(BF16)
        for turn in range(ROUNDS):
            b = 2 * head + turn
            spread = dot(info, one_hot(iota((WIDE, total), 0) == within + DH * turn))
            mine = iota((n, total), 0) == source
            place = 32.0 * spread[:n] + spread[n : 2 * n]
            token = 32.0 * spread[2 * n : 3 * n] + spread[3 * n :]
            place = jnp.sum(jnp.where(mine, place, 0.0), axis=0, keepdims=True) - 1.0
            token = jnp.sum(jnp.where(mine, token, 0.0), axis=0, keepdims=True)
            slot_row[b] = place.astype(I32)
            slot_col[b] = jnp.transpose(jnp.broadcast_to(place, (8, total)))[:, :1].astype(I32)
            comb = (source.astype(F32) * rows + token) * DH + within.astype(F32)

            def sort_tile(at, inner):
                chosen = iota((SPAN, total), 0) + at * SPAN == slot_row[b]
                got = recv1[head, :, turn * cap : (turn + 1) * cap, :].reshape(total, WIDE)
                moved = dot(one_hot(chosen), got)
                where = jnp.sum(jnp.where(chosen, comb, 0.0), axis=1, keepdims=True)
                where_int = where.astype(I32)
                sl = pl.ds(pl.multiple_of(at * SPAN, SPAN), SPAN)
                ext_sl = pl.ds(pl.multiple_of(at * SPAN + SPAN, SPAN), SPAN)
                ext[b, ext_sl, :] = moved.astype(BF16)
                place_col[b, sl, :] = where_int
                place_row[head, at + 1, turn : turn + 1, :] = to_row((where_int >> 6).astype(F32))
                home = (where_int >> (6 + log_rows)) * DH + (where_int & (DH - 1))
                dest_row[b, :, sl] = to_row(home.astype(F32)).astype(I32)
                query = jnp.where(low_half, moved, 0.0)
                mean = jnp.sum(query * query, axis=1, keepdims=True) * (1.0 / DH)
                inverse = lax.rsqrt(mean + 1e-06)
                inv_col[b, sl, :] = inverse
                keys[b, ext_sl, :] = (query * inverse).astype(BF16)
                return inner

            lax.fori_loop(0, nb, sort_tile, 0)
        for copy in boundary_copies(head):
            copy.start()
        return carry

    lax.fori_loop(0, PAIR, sort_head, 0)
    gather_step(3)

    own_token = iota((SPAN, 2 * SPAN), 1) == iota((SPAN, 2 * SPAN), 0) + SPAN

    def send_home(head, send, blocks, sums):
        def home_tile(at, inner):
            line = iota((tile, rows), 1)
            sl = pl.ds(pl.multiple_of(at * tile, EXTRA), tile)
            moved = [dot(one_hot(slot_col[2 * head + turn, sl, :] == line), blocks[2 * head + turn]) for turn in range(ROUNDS)]
            peers = pl.ds(at * PEERS, PEERS)
            if sums:
                send[head, peers, 0:cap, :] = (moved[0] + moved[1]).astype(BF16).reshape(PEERS, cap, WIDE)
            else:
                for turn in range(ROUNDS):
                    send[head, peers, turn * cap : (turn + 1) * cap, :] = (
                        moved[turn].astype(BF16).reshape(PEERS, cap, WIDE)
                    )
            return inner

        lax.fori_loop(0, tiles, home_tile, 0)

    def attend_head(head, carry):
        for copy in boundary_copies(head):
            copy.wait_recv()
        for turn in range(ROUNDS):
            b = 2 * head + turn
            query = jnp.where(low_half, ext[b, 0:SPAN, :].astype(F32), 0.0)
            mean = jnp.sum(query * query, axis=1, keepdims=True) * (1.0 / DH)
            keys[b, 0:SPAN, :] = (query * lax.rsqrt(mean + 1e-06)).astype(BF16)

        def attend_block(at, inner):
            first = pl.multiple_of(at * SPAN, SPAN)
            for turn in range(ROUNDS):
                b = 2 * head + turn
                window = ext[b, pl.ds(first, 2 * SPAN), :]
                query = ext[b, pl.ds(first + SPAN, SPAN), :]
                scores = dot_nt(query, keys[b, pl.ds(first, 2 * SPAN), :]) * (DH ** (-0.5))
                places = jnp.concatenate(
                    [place_row[head, at, turn : turn + 1, :], place_row[head, at + 1, turn : turn + 1, :]], axis=1
                )
                own_place = (place_col[b, pl.ds(first, SPAN), :] >> 6).astype(F32)
                scores = scores - jnp.where(own_token, 100000.0, 0.0)
                scores = scores - jnp.where(places > own_place, 1000000000.0, 0.0)
                top = jnp.max(scores, axis=1, keepdims=True)
                weight = jnp.exp(scores - top)
                norm = jnp.sum(weight, axis=1, keepdims=True)
                prob = (weight * (1.0 / norm)).astype(BF16)
                probs[b, pl.ds(first, SPAN), :] = prob
                log_row[b, :, pl.ds(first, SPAN)] = to_row(top + jnp.log(norm))
                result = dot(prob, window)
                if turn == 0:
                    result = swap_halves(result)
                result = jnp.where(low_half == (turn == 0), result, 0.0)
                outs[b, pl.ds(first, SPAN), :] = result.astype(BF16)
            return inner

        lax.fori_loop(0, nb, attend_block, 0)
        base = jnp.zeros((3 * n, WIDE), F32)
        for turn in range(ROUNDS):
            b = 2 * head + turn
            dest = dest_row[b]
            base = base + scatter_small(split3(log_row[b]), turn, dest >> 6, dest & (DH - 1))
        send2[head, :, cap : cap + EXTRA, :] = messages(3, base)
        send_home(head, send2, outs, True)
        exchange_start(send2.at[head], recv2.at[head], ssem.at[1, head], rsem.at[1, head])
        return carry

    lax.fori_loop(0, PAIR, attend_head, 0)
    for step in range(4, up_steps + 2):
        gather_step(step)
    for step in range(min(3, up_steps) + 1, 4):
        gather_step(step)

    def back_tile(at, carry):
        sl = pl.ds(pl.multiple_of(at * SPAN, SPAN), SPAN)
        value = jnp.zeros((SPAN, WIDE), F32)
        for chunk in range(z):
            value = value + dot_nt(full_grad[chunk, sl, :], w_ref[:, chunk * WIDE : (chunk + 1) * WIDE])
        value = value.astype(BF16).astype(F32)
        other = swap_halves(value)
        back[0, sl, :] = jnp.where(low_half, value, other)
        back[1, sl, :] = jnp.where(low_half, other, value)
        return carry

    lax.fori_loop(0, nb, back_tile, 0)

    def combine_head(head, carry):
        exchange_wait(recv2.at[head], rsem.at[1, head])
        parts = jnp.concatenate(
            message_parts(recv2[head, :, cap : cap + EXTRA, :], 3), axis=1
        ).astype(BF16)

        def combine_tile(at, inner):
            sl = pl.ds(pl.multiple_of(at * SPAN, SPAN), SPAN)
            got = recv2[head, :, 0:cap, :].reshape(total, WIDE)
            logs, moved = [], []
            for turn in range(ROUNDS):
                comb = comb_col[2 * head + turn, sl, :]
                target, spot = comb >> 6, comb & (DH - 1)
                logs.append(gather_small(parts, turn, target, spot))
                moved.append(dot(one_hot(iota((SPAN, total), 1) == target * cap + spot), got))
            top = jnp.maximum(logs[0], logs[1])
            raised = [jnp.exp(log - top) for log in logs]
            whole = raised[0] + raised[1]
            mixing = [r / whole for r in raised]
            mix = jnp.where(low_half, mixing[0], mixing[1])
            product = jnp.where(low_half, moved[0], moved[1]) * mix
            combined = product + swap_halves(product)
            attn[head, sl, :] = combined.astype(BF16)
            grad = back[head, sl, :]
            inside = 0.5 * jnp.sum(grad * combined, axis=1, keepdims=True)
            sent = grad * mix
            for turn in range(ROUNDS):
                b = 2 * head + turn
                grads[b, sl, :] = jnp.where(low_half == (turn == 0), sent, 0.0).astype(BF16)
                delta_row[b, :, sl] = to_row(mixing[turn] * inside)
            return inner

        lax.fori_loop(0, nb, combine_tile, 0)
        base = jnp.zeros((3 * n, WIDE), F32)
        for turn in range(ROUNDS):
            b = 2 * head + turn
            comb = comb_row[b]
            base = base + scatter_small(split3(delta_row[b]), turn, comb >> 6, comb & (DH - 1))
        send3[head, :, cap : cap + EXTRA, :] = messages(3, base)

        def pack_tile(at, inner):
            line = iota((tile, rows), 0) + at * tile
            moved = [dot(one_hot(line == spot_rows(2 * head + turn)), grads[2 * head + turn]) for turn in range(ROUNDS)]
            send3[head, pl.ds(at * PEERS, PEERS), 0:cap, :] = (
                (moved[0] + moved[1]).astype(BF16).reshape(PEERS, cap, WIDE)
            )
            return inner

        lax.fori_loop(0, tiles, pack_tile, 0)
        exchange_start(send3.at[head], recv3.at[head], ssem.at[2, head], rsem.at[2, head])
        return carry

    lax.fori_loop(0, PAIR, combine_head, 0)

    def term_tile(at, carry):
        sl = pl.ds(pl.multiple_of(at * SPAN, SPAN), SPAN)
        both = jnp.where(low_half, attn[0, sl, :].astype(F32), attn[1, sl, :].astype(F32))
        attn_t[:, sl] = jnp.transpose(both).astype(BF16)
        result = dot(both.astype(BF16), w_ref[...]).astype(BF16)
        for chunk in range(z):
            terms[chunk, sl, :] = result[:, chunk * WIDE : (chunk + 1) * WIDE]
        return carry

    lax.fori_loop(0, nb, term_tile, 0)

    def reduce_copy(going_up, step, first):
        sems = (rus, rur) if going_up else (rds, rdr)
        steps = up_steps if going_up else down_steps
        box = up_in if going_up else down_in
        if first:
            slot = lax.rem(me_h + steps, z) if going_up else lax.rem(me_h - steps + z, z)
            src = terms.at[slot]
        else:
            src = box.at[step - 2]
        return pltpu.make_async_remote_copy(
            src, box.at[step - 1], sems[0].at[step - 1], sems[1].at[step - 1],
            device_id={"head": up if going_up else down}, device_id_type=MESH,
        )

    def reduce_wait(going_up, step):
        box, sem = (up_in, rur) if going_up else (down_in, rdr)
        pltpu.make_async_copy(box.at[step - 1], box.at[step - 1], sem.at[step - 1]).wait()

    def reduce_step(step, ways):
        for going_up in ways:
            steps = up_steps if going_up else down_steps
            reduce_wait(going_up, step - 1)
            gone = steps - step + 1
            slot = lax.rem(me_h + gone, z) if going_up else lax.rem(me_h - gone + z, z)
            box = up_in if going_up else down_in
            box[step - 2] = (box[step - 2].astype(F32) + terms[slot].astype(F32)).astype(BF16)
            reduce_copy(going_up, step, False).start()

    reduce_copy(True, 1, True).start()
    if down_steps:
        reduce_copy(False, 1, True).start()

    pieces = n // z
    piece = WIDE // pieces
    for chunk in range(z):
        grad = dot(attn_t[...], full_grad[chunk]).astype(BF16)
        for at in range(pieces):
            wsend[chunk * pieces + at] = grad[at * piece : (at + 1) * piece]
    exchange_start(wsend, wrecv, wss.at[0], wrs.at[0])

    def spill_copy(head):
        return pltpu.make_async_remote_copy(
            spill_out.at[head], spill_in.at[head], psend.at[head], precv.at[head],
            device_id={"seq": before}, device_id_type=MESH,
        )

    early = up_steps >= 3 and down_steps >= 3

    def backward_head(head, carry):
        exchange_wait(recv3.at[head], rsem.at[2, head])
        parts = jnp.concatenate(
            message_parts(recv3[head, :, cap : cap + EXTRA, :], 3), axis=1
        ).astype(BF16)
        for turn in range(ROUNDS):
            b = 2 * head + turn

            def sort_tile(at, inner):
                sl = pl.ds(pl.multiple_of(at * SPAN, SPAN), SPAN)
                chosen = iota((SPAN, total), 0) + at * SPAN == slot_row[b]
                got = recv3[head, :, 0:cap, :].reshape(total, WIDE)
                moved = dot(one_hot(chosen), got)
                if turn == 0:
                    moved = swap_halves(moved)
                sorted_grad[b, sl, :] = jnp.where(low_half, 0.0, moved).astype(BF16)
                where = place_col[b, sl, :]
                delta_col[b, sl, :] = gather_small(parts, turn, where >> (6 + log_rows), where & (DH - 1))
                return inner

            lax.fori_loop(0, nb, sort_tile, 0)
            key_value[b, 0:SPAN, :] = jnp.zeros((SPAN, WIDE), F32)

        if early:
            reduce_step(head + 2, (True, False))

        def backward_block(at, inner):
            first = pl.multiple_of(at * SPAN, SPAN)
            sl = pl.ds(first, SPAN)
            nxt = pl.ds(first + SPAN, SPAN)
            for turn in range(ROUNDS):
                b = 2 * head + turn
                window = ext[b, pl.ds(first, 2 * SPAN), :]
                grad = sorted_grad[b, sl, :]
                prob = probs[b, sl, :]
                slope = prob.astype(F32) * (dot_nt(grad, window) - delta_col[b, sl, :])
                slope = slope.astype(BF16)
                query_part[b, sl, :] = dot(slope, keys[b, pl.ds(first, 2 * SPAN), :])
                query = jnp.where(low_half, ext[b, nxt, :].astype(F32) * (DH ** (-0.5)), 0.0).astype(BF16)
                both = dot_tn(
                    jnp.concatenate([slope, prob], axis=0), jnp.concatenate([query, grad], axis=0)
                )
                key_value[b, sl, :] += both[:SPAN]
                key_value[b, nxt, :] = both[SPAN:]

            @pl.when(at == 0)
            def _():
                for turn in range(ROUNDS):
                    spill_out[head, turn] = key_value[2 * head + turn, 0:SPAN, :].astype(BF16)
                spill_copy(head).start()

            return inner

        lax.fori_loop(0, nb, backward_block, 0)
        spill_copy(head).wait_recv()
        for turn in range(ROUNDS):
            key_value[2 * head + turn, rows : rows + SPAN, :] += spill_in[head, turn].astype(F32)

        def final_tile(at, inner):
            first = pl.multiple_of(at * SPAN, SPAN)
            sl = pl.ds(first, SPAN)
            nxt = pl.ds(first + SPAN, SPAN)
            for turn in range(ROUNDS):
                b = 2 * head + turn
                query = jnp.where(low_half, ext[b, nxt, :].astype(F32), 0.0)
                inverse = inv_col[b, sl, :]
                sums = key_value[b, nxt, :]
                mean = jnp.sum(query * sums, axis=1, keepdims=True) * (1.0 / DH)
                query_total = (
                    query_part[b, sl, :] * (DH ** (-0.5))
                    + inverse * sums
                    - query * (inverse * inverse * inverse) * mean
                )
                final[b, sl, :] = jnp.where(low_half, query_total, sums).astype(BF16)
            return inner

        lax.fori_loop(0, nb, final_tile, 0)
        send_home(head, send4, final, False)
        exchange_start(send4.at[head], recv4.at[head], ssem.at[3, head], rsem.at[3, head])
        return carry

    lax.fori_loop(0, PAIR, backward_head, 0)

    for step in range(4 if early else 2, up_steps + 1):
        reduce_step(step, (True,))
    for step in range(4 if early else 2, down_steps + 1):
        reduce_step(step, (False,))

    exchange_wait(wrecv, wrs.at[0])
    wsum[...] = jnp.broadcast_to(jnp.sum(wrecv[...].astype(F32), axis=0).astype(BF16)[None], wsum.shape)
    exchange_start(wsum, wall, wss.at[1], wrs.at[1])

    def final_head(head, carry):
        exchange_wait(recv4.at[head], rsem.at[3, head])

        def own_tile(at, inner):
            sl = pl.ds(pl.multiple_of(at * SPAN, SPAN), SPAN)
            value = jnp.zeros((SPAN, WIDE), F32)
            for turn in range(ROUNDS):
                comb = comb_col[2 * head + turn, sl, :]
                got = recv4[head, :, turn * cap : (turn + 1) * cap, :].reshape(total, WIDE)
                spot = (comb >> 6) * cap + (comb & (DH - 1))
                value = value + dot(one_hot(iota((SPAN, total), 1) == spot), got)
            own_grads[head, sl, :] = value
            return inner

        lax.fori_loop(0, nb, own_tile, 0)
        return carry

    lax.fori_loop(0, PAIR, final_head, 0)

    def output_tile(at, carry):
        sl = pl.ds(pl.multiple_of(at * SPAN, SPAN), SPAN)
        first, second = own_grads[0, sl, :], own_grads[1, sl, :]
        dq_ref[sl, :] = jnp.where(low_half, first, swap_halves(second)).astype(BF16)
        dv_ref[sl, :] = jnp.where(low_half, swap_halves(first), second).astype(BF16)
        return carry

    lax.fori_loop(0, nb, output_tile, 0)

    reduce_wait(True, up_steps)
    if down_steps:
        reduce_wait(False, down_steps)

    def result_tile(at, carry):
        sl = pl.ds(pl.multiple_of(at * SPAN, SPAN), SPAN)
        value = terms[me_h, sl, :].astype(F32) + up_in[up_steps - 1, sl, :].astype(F32)
        if down_steps:
            value = value + down_in[down_steps - 1, sl, :].astype(F32)
        out_ref[sl, :] = value.astype(BF16)
        return carry

    lax.fori_loop(0, nb, result_tile, 0)

    exchange_wait(wall, wrs.at[1])
    for chunk in range(z):
        for at in range(pieces):
            value = wall[chunk * pieces + at].astype(F32) * (n * rows) ** (-0.5)
            dw_ref[at * piece : (at + 1) * piece, chunk * WIDE : (chunk + 1) * WIDE] = value

    for head in range(PAIR):
        for at, send in enumerate((send1, send2, send3, send4)):
            exchange_drain(send.at[head], ssem.at[at, head])
        for copy in boundary_copies(head):
            copy.wait_send()
        spill_copy(head).wait_send()
    exchange_drain(wsend, wss.at[0])
    exchange_drain(wsum, wss.at[1])
    for going_up, steps in ((True, up_steps), (False, down_steps)):
        for step in range(1, steps + 1):
            gather_copy(going_up, step).wait_send()
            reduce_copy(going_up, step, step == 1).wait_send()


def per_device(n, z, queries, values, w_out, out_grad, slots):
    rows = queries.shape[0]
    cap = rows // n * 3 // 2
    total = n * cap
    nb = rows // SPAN
    up_steps = z // 2
    down_steps = max(z - 1 - up_steps, 1)
    piece = WIDE * z // n
    batch = ROUNDS * PAIR
    vmem = pltpu.VMEM
    dma = pltpu.SemaphoreType.DMA
    wide1 = (PAIR, n, 2 * cap + EXTRA, WIDE)
    wide2 = (PAIR, n, cap + EXTRA, WIDE)
    wide4 = (PAIR, n, 2 * cap, WIDE)
    scratch = [
        vmem(wide1, BF16), vmem(wide1, BF16),
        vmem(wide2, BF16), vmem(wide2, BF16),
        vmem(wide2, BF16), vmem(wide2, BF16),
        vmem(wide4, BF16), vmem(wide4, BF16),
        vmem((PAIR, rows, WIDE), BF16),
        vmem((batch, 1, rows), I32),
        vmem((batch, rows, 1), I32),
        vmem((batch, 1, total), I32),
        vmem((batch, total, 1), I32),
        vmem((batch, rows, 1), I32),
        vmem((batch, 1, rows), I32),
        vmem((PAIR, nb + 1, 8, SPAN), F32),
        vmem((batch, rows + SPAN, WIDE), BF16),
        vmem((batch, rows + SPAN, WIDE), BF16),
        vmem((batch, rows, 1), F32),
        vmem((batch, rows, 2 * SPAN), BF16),
        vmem((batch, 1, rows), F32),
        vmem((batch, rows, WIDE), BF16),
        vmem((PAIR, rows, WIDE), F32),
        vmem((PAIR, rows, WIDE), BF16),
        vmem((WIDE, rows), BF16),
        vmem((batch, rows, WIDE), BF16),
        vmem((batch, 1, rows), F32),
        vmem((batch, rows, WIDE), BF16),
        vmem((batch, rows, 1), F32),
        vmem((batch, rows, WIDE), F32),
        vmem((batch, rows + SPAN, WIDE), F32),
        vmem((batch, rows, WIDE), BF16),
        vmem((PAIR, ROUNDS, SPAN, WIDE), BF16),
        vmem((PAIR, ROUNDS, SPAN, WIDE), BF16),
        vmem((PAIR, rows, WIDE), F32),
        vmem((z, rows, WIDE), BF16),
        vmem((z, rows, WIDE), BF16),
        vmem((up_steps, rows, WIDE), BF16),
        vmem((down_steps, rows, WIDE), BF16),
        vmem((n, piece, WIDE), BF16),
        vmem((n, piece, WIDE), BF16),
        vmem((n, piece, WIDE), BF16),
        vmem((n, piece, WIDE), BF16),
        dma((4, PAIR)), dma((4, PAIR)),
        dma((PAIR, 3)), dma((PAIR, 3)),
        dma((PAIR,)), dma((PAIR,)),
        dma((up_steps,)), dma((up_steps,)), dma((down_steps,)), dma((down_steps,)),
        dma((up_steps,)), dma((up_steps,)), dma((down_steps,)), dma((down_steps,)),
        dma((2,)), dma((2,)),
    ]
    local = pl.BlockSpec(memory_space=pltpu.VMEM)
    return pl.pallas_call(
        functools.partial(kernel, n, z),
        out_shape=(
            jax.ShapeDtypeStruct((rows, WIDE), BF16),
            jax.ShapeDtypeStruct((rows, WIDE), BF16),
            jax.ShapeDtypeStruct((rows, WIDE), BF16),
            jax.ShapeDtypeStruct((WIDE, z * WIDE), F32),
        ),
        in_specs=[local] * 5,
        out_specs=[local] * 4,
        scratch_shapes=scratch,
        compiler_params=pltpu.CompilerParams(
            collective_id=0, has_side_effects=True, vmem_limit_bytes=62 * 1024 * 1024
        ),
    )(queries, values, w_out, out_grad, slots.reshape(batch, rows))


def solution(mesh):
    placed = (
        P("seq", "head"),
        P("seq", "head"),
        P("head", None),
        P("seq", "head"),
        P(None, "head", "seq"),
    )
    return jax.shard_map(
        functools.partial(per_device, mesh.shape["seq"], mesh.shape["head"]),
        mesh=mesh,
        in_specs=placed,
        out_specs=(P("seq", "head"), P("seq", "head"), P("seq", "head"), P("head", None)),
        check_vma=False,
    )
```

```python
import functools

import jax
import jax.numpy as jnp
from jax import lax
from jax.experimental import pallas as pl
from jax.experimental.pallas import tpu as pltpu
from jax.sharding import PartitionSpec as P

DH = 64
SPAN = 128
WIDE = 2 * DH
ROUNDS = 2
PAIR = 2
EXTRA = 16
PEERS = 4
MESH = pl.DeviceIdType.MESH
F32 = jnp.float32
BF16 = jnp.bfloat16
I32 = jnp.int32
I16 = jnp.int16
PACK = 16


def iota(shape, dim):
    return lax.broadcasted_iota(I32, shape, dim)


def one_hot(mask):
    return jnp.where(mask, 1.0, 0.0).astype(BF16)


def select16(masks, axis):
    one, zero = jnp.ones((), BF16), jnp.zeros((), BF16)
    return jnp.concatenate([jnp.where(mask, one, zero) for mask in masks], axis=axis)


def hot_rows(row, start, count):
    wide = (PACK, row.shape[1])
    near = jnp.broadcast_to(row - start, wide).astype(I16)
    line = iota(wide, 0).astype(I16)
    return select16([near == line + jnp.int16(at) for at in range(0, count, PACK)], 0)


def hot_cols(col, count):
    wide = (col.shape[0], SPAN)
    near = jnp.broadcast_to(col, wide).astype(I16)
    line = iota(wide, 1).astype(I16)
    return select16([near == line + jnp.int16(at) for at in range(0, count, SPAN)], 1)


def dot(a, b):
    return jnp.dot(a, b, preferred_element_type=F32)


def dot_nt(a, b):
    return lax.dot_general(a, b, (((1,), (1,)), ((), ())), preferred_element_type=F32)


def dot_tn(a, b):
    return lax.dot_general(a, b, (((0,), (0,)), ((), ())), preferred_element_type=F32)


def to_row(col):
    eye = iota((SPAN, SPAN), 0) == iota((SPAN, SPAN), 1)
    return jnp.sum(jnp.where(eye, col, 0.0), axis=0, keepdims=True)


def swap_halves(x):
    return pltpu.roll(x, DH, 1)


def split3(x):
    top = x.astype(BF16).astype(F32)
    rest = x - top
    middle = rest.astype(BF16).astype(F32)
    return [top, middle, rest - middle]


def kernel(
    n, z,
    q_ref, v_ref, w_ref, g_ref, slots_ref,
    out_ref, dq_ref, dv_ref, dw_ref,
    send1, recv1, send2, recv2, send3, recv3, send4, recv4,
    xqv, comb_row, comb_col, slot_row, slot_col, place_col, dest_row, place_row,
    ext, keys, inv_col, probs, log_row, outs, back, attn, attn_t, grads, delta_row,
    sorted_grad, delta_col, query_part, key_value, final, spill_out, spill_in, own_grads,
    full_grad, terms, up_in, down_in, wsend, wrecv, wsum, wall,
    ssem, rsem, bsend, brecv, psend, precv, gus, gur, gds, gdr, rus, rur, rds, rdr, wss, wrs,
):
    rows = q_ref.shape[0]
    share = rows // n
    cap = share * 3 // 2
    total = n * cap
    log_rows = rows.bit_length() - 1
    nb = rows // SPAN
    up_steps = z // 2
    down_steps = z - 1 - up_steps
    tiles = n // PEERS
    tile = PEERS * cap
    me = lax.axis_index("seq")
    me_h = lax.axis_index("head")
    up, down = lax.rem(me_h + 1, z), lax.rem(me_h + z - 1, z)
    after, before = lax.rem(me + 1, n), lax.rem(me + n - 1, n)

    barrier = pltpu.get_barrier_semaphore()

    def greet(off, carry):
        pl.semaphore_signal(barrier, inc=1, device_id={"seq": lax.rem(me + off, n)}, device_id_type=MESH)
        return carry

    lax.fori_loop(1, n, greet, 0)
    pl.semaphore_signal(barrier, inc=1, device_id={"head": up}, device_id_type=MESH)
    pl.semaphore_signal(barrier, inc=1, device_id={"head": down}, device_id_type=MESH)

    def exchange_start(send, recv, send_sem, recv_sem):
        def one(off, carry):
            peer = lax.rem(me + off, n)
            pltpu.make_async_remote_copy(
                send.at[peer], recv.at[me], send_sem, recv_sem, device_id={"seq": peer}, device_id_type=MESH
            ).start()
            return carry

        pltpu.make_async_copy(send.at[me], recv.at[me], recv_sem).start()
        lax.fori_loop(1, n, one, 0)

    def exchange_wait(recv, recv_sem):
        pltpu.make_async_copy(recv, recv, recv_sem).wait()

    def exchange_drain(send, send_sem):
        part = send.at[pl.ds(0, n - 1)]
        pltpu.make_async_copy(part, part, send_sem).wait()

    def gather_copy(going_up, step):
        if going_up:
            slot, sems, peer = lax.rem(me_h - (step - 1) + z, z), (gus, gur), up
        else:
            slot, sems, peer = lax.rem(me_h + (step - 1), z), (gds, gdr), down
        return pltpu.make_async_remote_copy(
            full_grad.at[slot], full_grad.at[slot], sems[0].at[step - 1], sems[1].at[step - 1],
            device_id={"head": peer}, device_id_type=MESH,
        )

    def gather_wait(going_up, step):
        slot = lax.rem(me_h - step + z, z) if going_up else lax.rem(me_h + step, z)
        sem = (gur if going_up else gdr).at[step - 1]
        pltpu.make_async_copy(full_grad.at[slot], full_grad.at[slot], sem).wait()

    def gather_step(step):
        for going_up, steps in ((True, up_steps), (False, down_steps)):
            if 1 < step <= steps + 1:
                gather_wait(going_up, step - 1)
            if step <= steps:
                gather_copy(going_up, step).start()

    def messages(comps, base):
        sub = iota((n, EXTRA, WIDE), 1)
        value = jnp.zeros((n, EXTRA, WIDE), F32)
        for at in range(comps):
            value = jnp.where(sub == at, base[at * n : (at + 1) * n][:, None, :], value)
        return value.astype(BF16)

    def message_parts(ref_value, comps):
        sub = iota((n, EXTRA, WIDE), 1)
        value = ref_value.astype(F32)
        return [jnp.sum(jnp.where(sub == at, value, 0.0), axis=1) for at in range(comps)]

    def scatter_small(parts, turn, target, spot):
        hot = jnp.where(iota((n, rows), 0) == target, 1.0, 0.0)
        left = jnp.concatenate([hot * part for part in parts], axis=0).astype(BF16)
        right = one_hot(iota((WIDE, rows), 0) == spot + DH * turn)
        return dot_nt(left, right)

    def gather_small(parts, turn, target, spot):
        hot = one_hot(iota((SPAN, n), 1) == target)
        wide = dot(hot, parts)
        value = wide[:, :WIDE] + wide[:, WIDE : 2 * WIDE] + wide[:, 2 * WIDE :]
        chosen = iota((SPAN, WIDE), 1) == spot + DH * turn
        return jnp.sum(jnp.where(chosen, value, 0.0), axis=1, keepdims=True)

    low_half = iota((SPAN, WIDE), 1) < DH

    for head in range(PAIR):
        for at in range(nb):
            sl = pl.ds(at * SPAN, SPAN)
            query = q_ref[sl, :].astype(F32)
            value = v_ref[sl, :].astype(F32)
            if head == 0:
                xqv[head, sl, :] = jnp.where(low_half, query, swap_halves(value)).astype(BF16)
            else:
                xqv[head, sl, :] = jnp.where(low_half, swap_halves(query), value).astype(BF16)
    full_grad[me_h] = g_ref[...]

    hots = []
    for head in range(PAIR):
        for turn in range(ROUNDS):
            slot = slots_ref[turn * PAIR + head : turn * PAIR + head + 1, :]
            hots.append(jnp.where(iota((n, rows), 0) == (slot >> log_rows), 1.0, 0.0))
    hot = jnp.concatenate(hots, axis=0)
    ahead = one_hot(iota((SPAN, SPAN), 0) < iota((SPAN, SPAN), 1))
    carry = jnp.zeros((4 * n, 1), F32)
    ranks = [[] for _ in range(4)]
    for at in range(nb):
        part = hot[:, at * SPAN : (at + 1) * SPAN]
        count = (dot(part.astype(BF16), ahead) + carry) * part
        carry = carry + jnp.sum(part, axis=1, keepdims=True)
        for b in range(4):
            ranks[b].append(jnp.sum(count[b * n : (b + 1) * n], axis=0, keepdims=True))
    position = iota((1, rows), 1)
    for head in range(PAIR):
        base = jnp.zeros((4 * n, WIDE), F32)
        for turn in range(ROUNDS):
            b = 2 * head + turn
            slot = slots_ref[turn * PAIR + head : turn * PAIR + head + 1, :]
            target = slot >> log_rows
            rank = jnp.concatenate(ranks[b], axis=1)
            rank_int = rank.astype(I32)
            comb = target * DH + rank_int
            comb_row[b] = comb
            comb_col[b] = jnp.transpose(jnp.broadcast_to(comb.astype(F32), (8, rows)))[:, :1].astype(I32)
            place = (slot & (rows - 1)) + 1
            parts = [place >> 5, place & 31, position >> 5, position & 31]
            base = base + scatter_small([p.astype(F32) for p in parts], turn, target, rank_int)
        send1[head, :, 2 * cap : 2 * cap + EXTRA, :] = messages(4, base)

    pl.semaphore_wait(barrier, n + 1)
    gather_step(1)

    def spot_rows(b):
        comb = comb_row[b]
        return (comb >> 6) * cap + (comb & (DH - 1))

    def pack_head(head, carry):
        def pack_tile(at, inner):
            for turn in range(ROUNDS):
                hot = hot_rows(spot_rows(2 * head + turn), at * tile, tile)
                moved = dot(hot, xqv[head]).astype(BF16).reshape(PEERS, cap, WIDE)
                send1[head, pl.ds(at * PEERS, PEERS), turn * cap : (turn + 1) * cap, :] = moved
            return inner

        lax.fori_loop(0, tiles, pack_tile, 0)
        exchange_start(send1.at[head], recv1.at[head], ssem.at[0, head], rsem.at[0, head])
        return carry

    lax.fori_loop(0, PAIR, pack_head, 0)
    gather_step(2)

    lanes = iota((1, total), 1)
    source = jnp.floor((lanes.astype(F32) + 0.5) * (1.0 / cap)).astype(I32)
    within = lanes - source * cap

    def boundary_copies(head):
        copies = []
        for turn in range(ROUNDS):
            b = 2 * head + turn
            copies.append((ext.at[b, pl.ds(rows, SPAN)], ext.at[b, pl.ds(0, SPAN)]))
        copies.append((place_row.at[head, nb], place_row.at[head, 0]))
        return [
            pltpu.make_async_remote_copy(
                src, dst, bsend.at[head, at], brecv.at[head, at], device_id={"seq": after}, device_id_type=MESH
            )
            for at, (src, dst) in enumerate(copies)
        ]

    def sort_head(head, carry):
        exchange_wait(recv1.at[head], rsem.at[0, head])
        info = message_parts(recv1[head, :, 2 * cap : 2 * cap + EXTRA, :], 4)
        info = jnp.concatenate(info, axis=0).astype(BF16)
        for turn in range(ROUNDS):
            b = 2 * head + turn
            spread = dot(info, one_hot(iota((WIDE, total), 0) == within + DH * turn))
            mine = iota((n, total), 0) == source
            place = 32.0 * spread[:n] + spread[n : 2 * n]
            token = 32.0 * spread[2 * n : 3 * n] + spread[3 * n :]
            place = jnp.sum(jnp.where(mine, place, 0.0), axis=0, keepdims=True) - 1.0
            token = jnp.sum(jnp.where(mine, token, 0.0), axis=0, keepdims=True)
            slot_row[b] = place.astype(I32)
            slot_col[b] = jnp.transpose(jnp.broadcast_to(place, (8, total)))[:, :1].astype(I32)
            comb = (source.astype(F32) * rows + token) * DH + within.astype(F32)

            def sort_tile(at, inner):
                chosen = iota((SPAN, total), 0) + at * SPAN == slot_row[b]
                got = recv1[head, :, turn * cap : (turn + 1) * cap, :].reshape(total, WIDE)
                moved = dot(one_hot(chosen), got)
                where = jnp.sum(jnp.where(chosen, comb, 0.0), axis=1, keepdims=True)
                where_int = where.astype(I32)
                sl = pl.ds(pl.multiple_of(at * SPAN, SPAN), SPAN)
                ext_sl = pl.ds(pl.multiple_of(at * SPAN + SPAN, SPAN), SPAN)
                ext[b, ext_sl, :] = moved.astype(BF16)
                place_col[b, sl, :] = where_int
                place_row[head, at + 1, turn : turn + 1, :] = to_row((where_int >> 6).astype(F32))
                home = (where_int >> (6 + log_rows)) * DH + (where_int & (DH - 1))
                dest_row[b, :, sl] = to_row(home.astype(F32)).astype(I32)
                query = jnp.where(low_half, moved, 0.0)
                mean = jnp.sum(query * query, axis=1, keepdims=True) * (1.0 / DH)
                inverse = lax.rsqrt(mean + 1e-06)
                inv_col[b, sl, :] = inverse
                keys[b, ext_sl, :] = (query * inverse).astype(BF16)
                return inner

            lax.fori_loop(0, nb, sort_tile, 0)
        for copy in boundary_copies(head):
            copy.start()
        return carry

    lax.fori_loop(0, PAIR, sort_head, 0)
    gather_step(3)

    own_token = iota((SPAN, 2 * SPAN), 1) == iota((SPAN, 2 * SPAN), 0) + SPAN

    def send_home(head, send, blocks, sums):
        def home_tile(at, inner):
            sl = pl.ds(pl.multiple_of(at * tile, EXTRA), tile)
            moved = [dot(hot_cols(slot_col[2 * head + turn, sl, :], rows), blocks[2 * head + turn]) for turn in range(ROUNDS)]
            peers = pl.ds(at * PEERS, PEERS)
            if sums:
                send[head, peers, 0:cap, :] = (moved[0] + moved[1]).astype(BF16).reshape(PEERS, cap, WIDE)
            else:
                for turn in range(ROUNDS):
                    send[head, peers, turn * cap : (turn + 1) * cap, :] = (
                        moved[turn].astype(BF16).reshape(PEERS, cap, WIDE)
                    )
            return inner

        lax.fori_loop(0, tiles, home_tile, 0)

    def attend_head(head, carry):
        for copy in boundary_copies(head):
            copy.wait_recv()
        for turn in range(ROUNDS):
            b = 2 * head + turn
            query = jnp.where(low_half, ext[b, 0:SPAN, :].astype(F32), 0.0)
            mean = jnp.sum(query * query, axis=1, keepdims=True) * (1.0 / DH)
            keys[b, 0:SPAN, :] = (query * lax.rsqrt(mean + 1e-06)).astype(BF16)

        def attend_block(at, inner):
            first = pl.multiple_of(at * SPAN, SPAN)
            for turn in range(ROUNDS):
                b = 2 * head + turn
                window = ext[b, pl.ds(first, 2 * SPAN), :]
                query = ext[b, pl.ds(first + SPAN, SPAN), :]
                scores = dot_nt(query, keys[b, pl.ds(first, 2 * SPAN), :]) * (DH ** (-0.5))
                places = jnp.concatenate(
                    [place_row[head, at, turn : turn + 1, :], place_row[head, at + 1, turn : turn + 1, :]], axis=1
                )
                own_place = (place_col[b, pl.ds(first, SPAN), :] >> 6).astype(F32)
                scores = scores - jnp.where(own_token, 100000.0, 0.0)
                scores = scores - jnp.where(places > own_place, 1000000000.0, 0.0)
                top = jnp.max(scores, axis=1, keepdims=True)
                weight = jnp.exp(scores - top)
                norm = jnp.sum(weight, axis=1, keepdims=True)
                prob = (weight * (1.0 / norm)).astype(BF16)
                probs[b, pl.ds(first, SPAN), :] = prob
                log_row[b, :, pl.ds(first, SPAN)] = to_row(top + jnp.log(norm))
                result = dot(prob, window)
                if turn == 0:
                    result = swap_halves(result)
                result = jnp.where(low_half == (turn == 0), result, 0.0)
                outs[b, pl.ds(first, SPAN), :] = result.astype(BF16)
            return inner

        lax.fori_loop(0, nb, attend_block, 0)
        base = jnp.zeros((3 * n, WIDE), F32)
        for turn in range(ROUNDS):
            b = 2 * head + turn
            dest = dest_row[b]
            base = base + scatter_small(split3(log_row[b]), turn, dest >> 6, dest & (DH - 1))
        send2[head, :, cap : cap + EXTRA, :] = messages(3, base)
        send_home(head, send2, outs, True)
        exchange_start(send2.at[head], recv2.at[head], ssem.at[1, head], rsem.at[1, head])
        return carry

    lax.fori_loop(0, PAIR, attend_head, 0)
    for step in range(4, up_steps + 2):
        gather_step(step)
    for step in range(min(3, up_steps) + 1, 4):
        gather_step(step)

    def back_tile(at, carry):
        sl = pl.ds(pl.multiple_of(at * SPAN, SPAN), SPAN)
        value = jnp.zeros((SPAN, WIDE), F32)
        for chunk in range(z):
            value = value + dot_nt(full_grad[chunk, sl, :], w_ref[:, chunk * WIDE : (chunk + 1) * WIDE])
        value = value.astype(BF16).astype(F32)
        other = swap_halves(value)
        back[0, sl, :] = jnp.where(low_half, value, other)
        back[1, sl, :] = jnp.where(low_half, other, value)
        return carry

    lax.fori_loop(0, nb, back_tile, 0)

    def combine_head(head, carry):
        exchange_wait(recv2.at[head], rsem.at[1, head])
        parts = jnp.concatenate(
            message_parts(recv2[head, :, cap : cap + EXTRA, :], 3), axis=1
        ).astype(BF16)

        def combine_tile(at, inner):
            sl = pl.ds(pl.multiple_of(at * SPAN, SPAN), SPAN)
            got = recv2[head, :, 0:cap, :].reshape(total, WIDE)
            logs, moved = [], []
            for turn in range(ROUNDS):
                comb = comb_col[2 * head + turn, sl, :]
                target, spot = comb >> 6, comb & (DH - 1)
                logs.append(gather_small(parts, turn, target, spot))
                moved.append(dot(hot_cols(target * cap + spot, total), got))
            top = jnp.maximum(logs[0], logs[1])
            raised = [jnp.exp(log - top) for log in logs]
            whole = raised[0] + raised[1]
            mixing = [r / whole for r in raised]
            mix = jnp.where(low_half, mixing[0], mixing[1])
            product = jnp.where(low_half, moved[0], moved[1]) * mix
            combined = product + swap_halves(product)
            attn[head, sl, :] = combined.astype(BF16)
            grad = back[head, sl, :]
            inside = 0.5 * jnp.sum(grad * combined, axis=1, keepdims=True)
            sent = grad * mix
            for turn in range(ROUNDS):
                b = 2 * head + turn
                grads[b, sl, :] = jnp.where(low_half == (turn == 0), sent, 0.0).astype(BF16)
                delta_row[b, :, sl] = to_row(mixing[turn] * inside)
            return inner

        lax.fori_loop(0, nb, combine_tile, 0)
        base = jnp.zeros((3 * n, WIDE), F32)
        for turn in range(ROUNDS):
            b = 2 * head + turn
            comb = comb_row[b]
            base = base + scatter_small(split3(delta_row[b]), turn, comb >> 6, comb & (DH - 1))
        send3[head, :, cap : cap + EXTRA, :] = messages(3, base)

        def pack_tile(at, inner):
            moved = [
                dot(hot_rows(spot_rows(2 * head + turn), at * tile, tile), grads[2 * head + turn])
                for turn in range(ROUNDS)
            ]
            send3[head, pl.ds(at * PEERS, PEERS), 0:cap, :] = (
                (moved[0] + moved[1]).astype(BF16).reshape(PEERS, cap, WIDE)
            )
            return inner

        lax.fori_loop(0, tiles, pack_tile, 0)
        exchange_start(send3.at[head], recv3.at[head], ssem.at[2, head], rsem.at[2, head])
        return carry

    lax.fori_loop(0, PAIR, combine_head, 0)

    def term_tile(at, carry):
        sl = pl.ds(pl.multiple_of(at * SPAN, SPAN), SPAN)
        both = jnp.where(low_half, attn[0, sl, :].astype(F32), attn[1, sl, :].astype(F32))
        attn_t[:, sl] = jnp.transpose(both).astype(BF16)
        result = dot(both.astype(BF16), w_ref[...]).astype(BF16)
        for chunk in range(z):
            terms[chunk, sl, :] = result[:, chunk * WIDE : (chunk + 1) * WIDE]
        return carry

    lax.fori_loop(0, nb, term_tile, 0)

    def reduce_copy(going_up, step, first):
        sems = (rus, rur) if going_up else (rds, rdr)
        steps = up_steps if going_up else down_steps
        box = up_in if going_up else down_in
        if first:
            slot = lax.rem(me_h + steps, z) if going_up else lax.rem(me_h - steps + z, z)
            src = terms.at[slot]
        else:
            src = box.at[step - 2]
        return pltpu.make_async_remote_copy(
            src, box.at[step - 1], sems[0].at[step - 1], sems[1].at[step - 1],
            device_id={"head": up if going_up else down}, device_id_type=MESH,
        )

    def reduce_wait(going_up, step):
        box, sem = (up_in, rur) if going_up else (down_in, rdr)
        pltpu.make_async_copy(box.at[step - 1], box.at[step - 1], sem.at[step - 1]).wait()

    def reduce_step(step, ways):
        for going_up in ways:
            steps = up_steps if going_up else down_steps
            reduce_wait(going_up, step - 1)
            gone = steps - step + 1
            slot = lax.rem(me_h + gone, z) if going_up else lax.rem(me_h - gone + z, z)
            box = up_in if going_up else down_in
            box[step - 2] = (box[step - 2].astype(F32) + terms[slot].astype(F32)).astype(BF16)
            reduce_copy(going_up, step, False).start()

    reduce_copy(True, 1, True).start()
    if down_steps:
        reduce_copy(False, 1, True).start()

    pieces = n // z
    piece = WIDE // pieces
    for chunk in range(z):
        grad = dot(attn_t[...], full_grad[chunk]).astype(BF16)
        for at in range(pieces):
            wsend[chunk * pieces + at] = grad[at * piece : (at + 1) * piece]
    exchange_start(wsend, wrecv, wss.at[0], wrs.at[0])

    def spill_copy(head):
        return pltpu.make_async_remote_copy(
            spill_out.at[head], spill_in.at[head], psend.at[head], precv.at[head],
            device_id={"seq": before}, device_id_type=MESH,
        )

    early = up_steps >= 3 and down_steps >= 3

    def backward_head(head, carry):
        exchange_wait(recv3.at[head], rsem.at[2, head])
        parts = jnp.concatenate(
            message_parts(recv3[head, :, cap : cap + EXTRA, :], 3), axis=1
        ).astype(BF16)
        for turn in range(ROUNDS):
            b = 2 * head + turn

            def sort_tile(at, inner):
                sl = pl.ds(pl.multiple_of(at * SPAN, SPAN), SPAN)
                got = recv3[head, :, 0:cap, :].reshape(total, WIDE)
                moved = dot(hot_rows(slot_row[b], at * SPAN, SPAN), got)
                if turn == 0:
                    moved = swap_halves(moved)
                sorted_grad[b, sl, :] = jnp.where(low_half, 0.0, moved).astype(BF16)
                where = place_col[b, sl, :]
                delta_col[b, sl, :] = gather_small(parts, turn, where >> (6 + log_rows), where & (DH - 1))
                return inner

            lax.fori_loop(0, nb, sort_tile, 0)
            key_value[b, 0:SPAN, :] = jnp.zeros((SPAN, WIDE), F32)

        if early:
            reduce_step(head + 2, (True, False))

        def backward_block(at, inner):
            first = pl.multiple_of(at * SPAN, SPAN)
            sl = pl.ds(first, SPAN)
            nxt = pl.ds(first + SPAN, SPAN)
            for turn in range(ROUNDS):
                b = 2 * head + turn
                window = ext[b, pl.ds(first, 2 * SPAN), :]
                grad = sorted_grad[b, sl, :]
                prob = probs[b, sl, :]
                slope = prob.astype(F32) * (dot_nt(grad, window) - delta_col[b, sl, :])
                slope = slope.astype(BF16)
                query_part[b, sl, :] = dot(slope, keys[b, pl.ds(first, 2 * SPAN), :])
                query = jnp.where(low_half, ext[b, nxt, :].astype(F32) * (DH ** (-0.5)), 0.0).astype(BF16)
                both = dot_tn(
                    jnp.concatenate([slope, prob], axis=0), jnp.concatenate([query, grad], axis=0)
                )
                key_value[b, sl, :] += both[:SPAN]
                key_value[b, nxt, :] = both[SPAN:]

            @pl.when(at == 0)
            def _():
                for turn in range(ROUNDS):
                    spill_out[head, turn] = key_value[2 * head + turn, 0:SPAN, :].astype(BF16)
                spill_copy(head).start()

            return inner

        lax.fori_loop(0, nb, backward_block, 0)
        spill_copy(head).wait_recv()
        for turn in range(ROUNDS):
            key_value[2 * head + turn, rows : rows + SPAN, :] += spill_in[head, turn].astype(F32)

        def final_tile(at, inner):
            first = pl.multiple_of(at * SPAN, SPAN)
            sl = pl.ds(first, SPAN)
            nxt = pl.ds(first + SPAN, SPAN)
            for turn in range(ROUNDS):
                b = 2 * head + turn
                query = jnp.where(low_half, ext[b, nxt, :].astype(F32), 0.0)
                inverse = inv_col[b, sl, :]
                sums = key_value[b, nxt, :]
                mean = jnp.sum(query * sums, axis=1, keepdims=True) * (1.0 / DH)
                query_total = (
                    query_part[b, sl, :] * (DH ** (-0.5))
                    + inverse * sums
                    - query * (inverse * inverse * inverse) * mean
                )
                final[b, sl, :] = jnp.where(low_half, query_total, sums).astype(BF16)
            return inner

        lax.fori_loop(0, nb, final_tile, 0)
        send_home(head, send4, final, False)
        exchange_start(send4.at[head], recv4.at[head], ssem.at[3, head], rsem.at[3, head])
        return carry

    lax.fori_loop(0, PAIR, backward_head, 0)

    for step in range(4 if early else 2, up_steps + 1):
        reduce_step(step, (True,))
    for step in range(4 if early else 2, down_steps + 1):
        reduce_step(step, (False,))

    exchange_wait(wrecv, wrs.at[0])
    wsum[...] = jnp.broadcast_to(jnp.sum(wrecv[...].astype(F32), axis=0).astype(BF16)[None], wsum.shape)
    exchange_start(wsum, wall, wss.at[1], wrs.at[1])

    def final_head(head, carry):
        exchange_wait(recv4.at[head], rsem.at[3, head])

        def own_tile(at, inner):
            sl = pl.ds(pl.multiple_of(at * SPAN, SPAN), SPAN)
            value = jnp.zeros((SPAN, WIDE), F32)
            for turn in range(ROUNDS):
                comb = comb_col[2 * head + turn, sl, :]
                got = recv4[head, :, turn * cap : (turn + 1) * cap, :].reshape(total, WIDE)
                spot = (comb >> 6) * cap + (comb & (DH - 1))
                value = value + dot(hot_cols(spot, total), got)
            own_grads[head, sl, :] = value
            return inner

        lax.fori_loop(0, nb, own_tile, 0)
        return carry

    lax.fori_loop(0, PAIR, final_head, 0)

    def output_tile(at, carry):
        sl = pl.ds(pl.multiple_of(at * SPAN, SPAN), SPAN)
        first, second = own_grads[0, sl, :], own_grads[1, sl, :]
        dq_ref[sl, :] = jnp.where(low_half, first, swap_halves(second)).astype(BF16)
        dv_ref[sl, :] = jnp.where(low_half, swap_halves(first), second).astype(BF16)
        return carry

    lax.fori_loop(0, nb, output_tile, 0)

    reduce_wait(True, up_steps)
    if down_steps:
        reduce_wait(False, down_steps)

    def result_tile(at, carry):
        sl = pl.ds(pl.multiple_of(at * SPAN, SPAN), SPAN)
        value = terms[me_h, sl, :].astype(F32) + up_in[up_steps - 1, sl, :].astype(F32)
        if down_steps:
            value = value + down_in[down_steps - 1, sl, :].astype(F32)
        out_ref[sl, :] = value.astype(BF16)
        return carry

    lax.fori_loop(0, nb, result_tile, 0)

    exchange_wait(wall, wrs.at[1])
    for chunk in range(z):
        for at in range(pieces):
            value = wall[chunk * pieces + at].astype(F32) * (n * rows) ** (-0.5)
            dw_ref[at * piece : (at + 1) * piece, chunk * WIDE : (chunk + 1) * WIDE] = value

    for head in range(PAIR):
        for at, send in enumerate((send1, send2, send3, send4)):
            exchange_drain(send.at[head], ssem.at[at, head])
        for copy in boundary_copies(head):
            copy.wait_send()
        spill_copy(head).wait_send()
    exchange_drain(wsend, wss.at[0])
    exchange_drain(wsum, wss.at[1])
    for going_up, steps in ((True, up_steps), (False, down_steps)):
        for step in range(1, steps + 1):
            gather_copy(going_up, step).wait_send()
            reduce_copy(going_up, step, step == 1).wait_send()


def per_device(n, z, queries, values, w_out, out_grad, slots):
    rows = queries.shape[0]
    cap = rows // n * 3 // 2
    total = n * cap
    nb = rows // SPAN
    up_steps = z // 2
    down_steps = max(z - 1 - up_steps, 1)
    piece = WIDE * z // n
    batch = ROUNDS * PAIR
    vmem = pltpu.VMEM
    dma = pltpu.SemaphoreType.DMA
    wide1 = (PAIR, n, 2 * cap + EXTRA, WIDE)
    wide2 = (PAIR, n, cap + EXTRA, WIDE)
    wide4 = (PAIR, n, 2 * cap, WIDE)
    scratch = [
        vmem(wide1, BF16), vmem(wide1, BF16),
        vmem(wide2, BF16), vmem(wide2, BF16),
        vmem(wide2, BF16), vmem(wide2, BF16),
        vmem(wide4, BF16), vmem(wide4, BF16),
        vmem((PAIR, rows, WIDE), BF16),
        vmem((batch, 1, rows), I32),
        vmem((batch, rows, 1), I32),
        vmem((batch, 1, total), I32),
        vmem((batch, total, 1), I32),
        vmem((batch, rows, 1), I32),
        vmem((batch, 1, rows), I32),
        vmem((PAIR, nb + 1, 8, SPAN), F32),
        vmem((batch, rows + SPAN, WIDE), BF16),
        vmem((batch, rows + SPAN, WIDE), BF16),
        vmem((batch, rows, 1), F32),
        vmem((batch, rows, 2 * SPAN), BF16),
        vmem((batch, 1, rows), F32),
        vmem((batch, rows, WIDE), BF16),
        vmem((PAIR, rows, WIDE), F32),
        vmem((PAIR, rows, WIDE), BF16),
        vmem((WIDE, rows), BF16),
        vmem((batch, rows, WIDE), BF16),
        vmem((batch, 1, rows), F32),
        vmem((batch, rows, WIDE), BF16),
        vmem((batch, rows, 1), F32),
        vmem((batch, rows, WIDE), F32),
        vmem((batch, rows + SPAN, WIDE), F32),
        vmem((batch, rows, WIDE), BF16),
        vmem((PAIR, ROUNDS, SPAN, WIDE), BF16),
        vmem((PAIR, ROUNDS, SPAN, WIDE), BF16),
        vmem((PAIR, rows, WIDE), F32),
        vmem((z, rows, WIDE), BF16),
        vmem((z, rows, WIDE), BF16),
        vmem((up_steps, rows, WIDE), BF16),
        vmem((down_steps, rows, WIDE), BF16),
        vmem((n, piece, WIDE), BF16),
        vmem((n, piece, WIDE), BF16),
        vmem((n, piece, WIDE), BF16),
        vmem((n, piece, WIDE), BF16),
        dma((4, PAIR)), dma((4, PAIR)),
        dma((PAIR, 3)), dma((PAIR, 3)),
        dma((PAIR,)), dma((PAIR,)),
        dma((up_steps,)), dma((up_steps,)), dma((down_steps,)), dma((down_steps,)),
        dma((up_steps,)), dma((up_steps,)), dma((down_steps,)), dma((down_steps,)),
        dma((2,)), dma((2,)),
    ]
    local = pl.BlockSpec(memory_space=pltpu.VMEM)
    return pl.pallas_call(
        functools.partial(kernel, n, z),
        out_shape=(
            jax.ShapeDtypeStruct((rows, WIDE), BF16),
            jax.ShapeDtypeStruct((rows, WIDE), BF16),
            jax.ShapeDtypeStruct((rows, WIDE), BF16),
            jax.ShapeDtypeStruct((WIDE, z * WIDE), F32),
        ),
        in_specs=[local] * 5,
        out_specs=[local] * 4,
        scratch_shapes=scratch,
        compiler_params=pltpu.CompilerParams(
            collective_id=0, has_side_effects=True, vmem_limit_bytes=62 * 1024 * 1024
        ),
    )(queries, values, w_out, out_grad, slots.reshape(batch, rows))


def solution(mesh):
    placed = (
        P("seq", "head"),
        P("seq", "head"),
        P("head", None),
        P("seq", "head"),
        P(None, "head", "seq"),
    )
    return jax.shard_map(
        functools.partial(per_device, mesh.shape["seq"], mesh.shape["head"]),
        mesh=mesh,
        in_specs=placed,
        out_specs=(P("seq", "head"), P("seq", "head"), P("seq", "head"), P("head", None)),
        check_vma=False,
    )
```
